32 devices in a mesh: sub: 16 (over z, y, core), coarse: 2 (over x).
Axes of the slice: x: 2, y: 2, z: 4, core: 2. Of those that a mesh axis runs over, the one named last changes fastest.
Arguments:
- loads: float32 [32, 32, 32, 128], P(('sub', 'coarse')), may hold values from -6 to 6
- diag_blocks: float32 [32, 32, 128, 128], P(('sub', 'coarse')), may hold values from -0.2 to 6.2
- off_blocks: float32 [32, 32, 2, 128, 128], P(('sub', 'coarse')), may hold values from -0.25 to 0.25
- off_index: int32 [32, 32, 2], P(('sub', 'coarse')), may hold values from 0 to 31, as said below
- couple_blocks: float32 [32, 2, 128, 128], P(('sub', 'coarse')), may hold values from -0.5 to 0.5
- basis: float32 [32, 128, 32, 128], P(('sub', 'coarse')), may hold values from -0.09375 to 0.09375
- coarse_blocks: float32 [32, 6, 128, 128], P(('sub', 'coarse')), may hold values from -0.21875 to 0.21875
- coarse_index: int32 [32, 6], P(('sub', 'coarse')), may hold values from 0 to 31, as said below
Outputs:
- solution: float32 [32, 32, 32, 128], P(('sub', 'coarse'))
- residual: float32 [32, 32, 32, 128], P(('sub', 'coarse'))
The draws below stay inside these ranges and needn't reach their ends.
Inputs may be any that keep to these rules, and one draw needn't show every extreme that they name: `off_index`: the 2 entries of a block row name different blocks of the same subdomain, none of them the row's own block. `coarse_index`: the 6 entries of a row name different subdomains, the first being the row's own subdomain g and the second g - 1 counted round.
All inputs are finite; a program needn't handle non-finite values.
Results may differ from the reference program's by a relative error of at most 0.0001.
Values sent between devices are 32-bit elements; how exact they have to be, the bound alone decides.
A program may use at most 128 MiB of HBM per device.

```python
import jax
import jax.numpy as jnp
from jax import lax

N_LOC = 4096
BS = 128
NB = 32
K = 128
COLS = 32
NOFF = 2
NCB = 6
ORDER = 5
ITERS = 2
SUBS = 32
N_SUB = 16
N_COARSE = 2


def draw_diag_blocks(key, part):
    key_diag, key_rest = jax.random.split(jax.random.fold_in(key, 11))
    values = jax.random.uniform(key_diag, (SUBS, NB, BS), jnp.float32, 3.0, 6.0)
    spread = 0.5 / BS ** 0.5
    rest = jax.random.normal(key_rest, (SUBS, NB, BS, BS), jnp.float32) * spread
    rest = jnp.clip(rest, -0.2, 0.2)
    return rest + values[..., None] * jnp.eye(BS, dtype=jnp.float32)


def draw_off_index(key, part):
    steps = jax.random.randint(jax.random.fold_in(key, 23), (SUBS, NB, NOFF), 1, NB // NOFF)
    offsets = jnp.cumsum(steps, axis=2)
    rows = jnp.arange(NB, dtype=jnp.int32)[None, :, None]
    return ((rows + offsets) % NB).astype(jnp.int32)


def draw_coarse_index(key, part):
    steps = jax.random.randint(jax.random.fold_in(key, 37), (SUBS, NCB - 2), 1, SUBS // NCB)
    rest = jnp.cumsum(steps, axis=1).astype(jnp.int32)
    own = jnp.zeros((SUBS, 1), jnp.int32)
    before = jnp.full((SUBS, 1), SUBS - 1, jnp.int32)
    offsets = jnp.concatenate([own, before, rest], axis=1)
    rows = jnp.arange(SUBS, dtype=jnp.int32)[:, None]
    return ((rows + offsets) % SUBS).astype(jnp.int32)


def shard_levels(stream_key, shape, cuts, low, largest):
    factor_of = 1.0
    for axis_at, parts in cuts:
        heights = jax.random.uniform(jax.random.fold_in(jax.random.fold_in(stream_key, 6), axis_at), (parts,), jnp.float32, low / len(cuts), largest / len(cuts))
        factor_of = factor_of * jnp.repeat(jnp.exp(heights), shape[axis_at] // parts).reshape((-1,) + (1,) * (len(shape) - 1 - axis_at))
    return factor_of


def scatter_about(key, shape, scale, bound, shards=(), kind=jnp.bfloat16):
    factor_of = shard_levels(key, shape, shards, -0.22, 0.18) if shards else 1.0
    drawn = jax.random.normal(key, shape, jnp.float32) * scale * factor_of
    return jnp.minimum(jnp.maximum(drawn, -bound), bound).astype(kind)


def setup_inputs(seed: int = 0) -> dict:
    streams_of = jax.random.split(jax.random.key(seed), 9)
    loads = scatter_about(streams_of[0], (SUBS, COLS, NB, BS), 1.0, 6.0, ((0, 32),), jnp.float32)
    diag_blocks = draw_diag_blocks(jax.random.fold_in(streams_of[8], 71), 0)
    off_blocks = scatter_about(streams_of[2], (SUBS, NB, NOFF, BS, BS), (4 * BS) ** -0.5, 0.25, ((0, 32),), jnp.float32)
    off_index = draw_off_index(jax.random.fold_in(streams_of[8], 71), 0)
    couple_blocks = scatter_about(streams_of[4], (SUBS, 2, BS, BS), BS ** -0.5, 0.5, ((0, 32),), jnp.float32)
    basis = scatter_about(streams_of[5], (SUBS, K, NB, BS), N_LOC ** -0.5, 0.09375, ((0, 32),), jnp.float32)
    coarse_blocks = scatter_about(streams_of[6], (SUBS, NCB, K, K), (NCB * K) ** -0.5, 0.21875, ((0, 32),), jnp.float32)
    coarse_index = draw_coarse_index(jax.random.fold_in(streams_of[8], 71), 0)
    return dict(loads=loads, diag_blocks=diag_blocks, off_blocks=off_blocks, off_index=off_index, couple_blocks=couple_blocks, basis=basis, coarse_blocks=coarse_blocks, coarse_index=coarse_index)


highest = lax.Precision.HIGHEST
theta_mid = 5.0
delta_half = 4.0


def from_left(value):
    shaped = value.reshape((N_SUB, N_COARSE) + value.shape[1:])
    shaped = jnp.concatenate([jnp.zeros_like(shaped[:1]), shaped[:-1]], axis=0)
    return shaped.reshape(value.shape)


def from_right(value):
    shaped = value.reshape((N_SUB, N_COARSE) + value.shape[1:])
    shaped = jnp.concatenate([shaped[1:], jnp.zeros_like(shaped[:1])], axis=0)
    return shaped.reshape(value.shape)


def own_rows(own, left_block, right_block, diag, offs, index, couple):
    result = jnp.einsum("cbk,bik->cbi", own, diag, precision=highest)
    picked = jnp.take(own, index, axis=1)
    result = result + jnp.einsum("cbjk,bjik->cbi", picked, offs, precision=highest)
    first = result[:, 0] + jnp.einsum("ck,ik->ci", left_block, couple[0], precision=highest)
    last = result[:, -1] + jnp.einsum("ck,ik->ci", right_block, couple[1], precision=highest)
    return result.at[:, 0].set(first).at[:, -1].set(last)


def padded_rows(padded, diag, offs, index, couple, left_diag, left_up, right_diag, right_low):
    middle = own_rows(padded[:, 1:-1], padded[:, 0], padded[:, -1], diag, offs, index, couple)
    top = jnp.einsum("ck,ik->ci", padded[:, 0], left_diag, precision=highest)
    top = top + jnp.einsum("ck,ik->ci", padded[:, 1], left_up, precision=highest)
    bottom = jnp.einsum("ck,ik->ci", padded[:, -1], right_diag, precision=highest)
    bottom = bottom + jnp.einsum("ck,ik->ci", padded[:, -2], right_low, precision=highest)
    return jnp.concatenate([top[:, None], middle, bottom[:, None]], axis=1)


def chebyshev(padded, diag, offs, index, couple, left_diag, left_up, right_diag, right_low):
    sigma = theta_mid / delta_half
    rho_now = 1.0 / sigma
    direction = padded / theta_mid
    smooth = jnp.zeros_like(padded)
    for step in range(ORDER):
        smooth = smooth + direction
        if step + 1 < ORDER:
            misfit = padded - padded_rows(smooth, diag, offs, index, couple, left_diag, left_up, right_diag, right_low)
            rho_next = 1.0 / (2.0 * sigma - rho_now)
            direction = rho_next * rho_now * direction + (2.0 * rho_next / delta_half) * misfit
            rho_now = rho_next
    return smooth


def reference(loads, diag_blocks, off_blocks, off_index, couple_blocks, basis, coarse_blocks, coarse_index):
    left_diag = from_left(diag_blocks[:, -1])
    left_up = from_left(couple_blocks[:, 1])
    right_diag = from_right(diag_blocks[:, 0])
    right_low = from_right(couple_blocks[:, 0])
    solution = jnp.zeros_like(loads)
    resid = loads
    for step in range(ITERS):
        padded = jnp.concatenate([from_left(resid[:, :, -1])[:, :, None], resid, from_right(resid[:, :, 0])[:, :, None]], axis=2)
        smooth = jax.vmap(chebyshev)(padded, diag_blocks, off_blocks, off_index, couple_blocks, left_diag, left_up, right_diag, right_low)
        coeffs = jnp.einsum("scbi,skbi->sck", resid, basis, precision=highest)
        picked = coeffs[coarse_index]
        coarse_sol = jnp.einsum("sjck,sjik->sci", picked, coarse_blocks, precision=highest)
        edge = smooth[:, :, 1:-1] + jnp.einsum("sck,skbi->scbi", coarse_sol, basis, precision=highest)
        first = edge[:, :, 0] + from_left(smooth[:, :, -1])
        last = edge[:, :, -1] + from_right(smooth[:, :, 0])
        change = edge.at[:, :, 0].set(first).at[:, :, -1].set(last)
        solution = solution + change
        applied = jax.vmap(own_rows)(change, from_left(change[:, :, -1]), from_right(change[:, :, 0]), diag_blocks, off_blocks, off_index, couple_blocks)
        resid = resid - applied
    return solution, resid
```

```python
import functools

import jax
import jax.numpy as jnp
from jax import lax
from jax.experimental import pallas as pl
from jax.experimental.pallas import tpu as pltpu
from jax.sharding import PartitionSpec as P

ORDER = 5
ITERS = 2
THETA = 5.0
DELTA = 4.0
F32 = jnp.float32
BF16 = jnp.bfloat16
MESH = pl.DeviceIdType.MESH
CHUNKS = 4
BGROUP = 4


def cheb_coefs():
    sigma = THETA / DELTA
    rho = 1.0 / sigma
    out = []
    for _ in range(ORDER - 1):
        nxt = 1.0 / (2.0 * sigma - rho)
        out.append((nxt * rho, 2.0 * nxt / DELTA))
        rho = nxt
    return out


def halves(v):
    hi = v.astype(BF16)
    lo = (v - hi.astype(F32)).astype(BF16)
    return hi, lo


def dot_nt(x, w):
    return lax.dot_general(x, w, (((1,), (1,)), ((), ())), preferred_element_type=F32)


def dot_nn(x, w):
    return lax.dot_general(x, w, (((1,), (0,)), ((), ())), preferred_element_type=F32)


def kernel(
    ns, nc, ny, nb, cols, bs, ncb,
    loads, diag, offs, oidx, couple, basis, cblk, cidx,
    sol, res,
    f_loads, f_diag, f_offs, f_couple, f_basis, f_cblk,
    w, wc, wt, bw, bt, cw,
    r, d, z, sv, ua, ub, ur,
    gath0, gath1, op_in, r_in, e_in, e_out,
    lsem, wsem, osem, op_s, op_r, rh_s, rh_r, e_s, e_r,
    line_s, line_r, side_s, side_r, pass_s, pass_r, mate_s, mate_r,
):
    me_s = lax.axis_index("sub")
    me_x = lax.axis_index("coarse")
    core = lax.rem(me_s, 2)
    h = me_s // 2
    nz = ns // 2 // ny
    nq = ny * nc
    hz = h // ny
    q = lax.rem(h, ny) * nc + me_x
    partner = me_s + 1 - 2 * core
    has_l = me_s > 0
    has_r = me_s < ns - 1
    nb2 = nb // 2
    left, right = nb, nb + 1
    chunk = nb // CHUNKS

    ld = [
        pltpu.make_async_copy(loads, f_loads, lsem.at[0]),
        pltpu.make_async_copy(basis, f_basis, lsem.at[1]),
        pltpu.make_async_copy(couple, f_couple, lsem.at[2]),
        pltpu.make_async_copy(cblk, f_cblk, lsem.at[3]),
    ]
    ldw = [
        [
            pltpu.make_async_copy(src.at[span], dst.at[span], wsem.at[i, c])
            for i, (src, dst) in enumerate(((diag, f_diag), (offs, f_offs)))
        ]
        for c, span in enumerate(pl.ds(c * chunk, chunk) for c in range(CHUNKS))
    ]
    ld[0].start()
    ld[1].start()
    ld[2].start()
    for pair in ldw:
        for c in pair:
            c.start()
    ld[3].start()

    def remote(src, dst, ss, rs, s, x):
        return pltpu.make_async_remote_copy(
            src_ref=src, dst_ref=dst, send_sem=ss, recv_sem=rs,
            device_id={"sub": s, "coarse": x}, device_id_type=MESH,
        )

    barrier = pltpu.get_barrier_semaphore()

    def greet(s, x):
        pl.semaphore_signal(
            barrier, inc=1, device_id={"sub": s, "coarse": x}, device_id_type=MESH
        )

    def on_line(k):
        return core + 2 * (lax.rem(hz + k, nz) * ny + lax.rem(h, ny)), me_x

    def on_side(m):
        to = lax.rem(q + m, nq)
        return core + 2 * (hz * ny + to // nc), lax.rem(to, nc)

    for k in range(1, nz):
        greet(*on_line(k))
    for m in range(1, nq):
        greet(*on_side(m))

    @pl.when(has_l)
    def _():
        greet(me_s - 1, me_x)

    @pl.when(has_r)
    def _():
        greet(me_s + 1, me_x)

    for side, has in ((0, has_l), (1, has_r)):

        @pl.when(jnp.logical_not(has))
        def _():
            op_in[side] = jnp.zeros_like(op_in[side])
            for it in range(ITERS):
                r_in[it, side] = jnp.zeros_like(r_in[it, side])
                e_in[it, side] = jnp.zeros_like(e_in[it, side])

    def put(ref, b, v):
        hi, lo = halves(v)
        ref[b, 0:cols, :] = hi
        ref[b, cols : 2 * cols, :] = lo

    def fold(o):
        return (o[:cols, :bs] + o[:cols, bs:]) + (o[cols:, :bs] + o[cols:, bs:])

    ld[0].wait()

    for b in range(nb):
        v = f_loads[pl.ds(b, cols, stride=nb), :]
        r[b] = v
        put(ur, b, v)
    pl.semaphore_wait(
        barrier, nz - 1 + nq - 1 + has_l.astype(jnp.int32) + has_r.astype(jnp.int32)
    )

    def op_copies(to_left):
        b = 0 if to_left else nb - 1
        side = 1 if to_left else 0
        s = me_s - 1 if to_left else me_s + 1
        return [
            remote(diag.at[b], op_in.at[side, 0], op_s.at[side, 0], op_r.at[side, 0], s, me_x),
            remote(
                couple.at[0 if to_left else 1], op_in.at[side, 1],
                op_s.at[side, 1], op_r.at[side, 1], s, me_x,
            ),
        ]

    def r_copy(it, to_left):
        b = 0 if to_left else nb - 1
        side = 1 if to_left else 0
        s = me_s - 1 if to_left else me_s + 1
        return [remote(r.at[b], r_in.at[it, side], rh_s.at[it, side], rh_r.at[it, side], s, me_x)]

    def e_copy(it, to_left):
        side = 1 if to_left else 0
        s = me_s - 1 if to_left else me_s + 1
        return [
            remote(
                e_out.at[it, side], e_in.at[it, side], e_s.at[it, side], e_r.at[it, side], s, me_x
            )
        ]

    def start_both(make):
        @pl.when(has_l)
        def _():
            for c in make(True):
                c.start()

        @pl.when(has_r)
        def _():
            for c in make(False):
                c.start()

    def wait_both(make):
        @pl.when(has_l)
        def _():
            for c in make(True):
                c.wait_send()
            for c in make(False):
                c.wait_recv()

        @pl.when(has_r)
        def _():
            for c in make(False):
                c.wait_send()
            for c in make(True):
                c.wait_recv()

    start_both(functools.partial(r_copy, 0))
    start_both(op_copies)
    ld[1].wait()

    def init_basis(g, carry):
        for p in range(BGROUP):
            t = g * BGROUP + p
            for e in range(2):
                hi, lo = halves(f_basis[pl.ds(2 * t + e, bs, stride=nb), :])
                cut = slice(e * bs, (e + 1) * bs)
                bw[t, 0:bs, cut] = hi
                bw[t, bs : 2 * bs, cut] = lo
                bt[t, cut, 0:bs] = hi.T
                bt[t, cut, bs : 2 * bs] = lo.T
        return carry

    lax.fori_loop(0, nb2 // BGROUP, init_basis, 0)

    gath = (gath0, gath1)

    def line(it, k):
        mine = gath[it].at[core, hz, q]
        return remote(mine, mine, line_s.at[it, k - 1], line_r.at[it, k - 1], *on_line(k))

    def side(it, m):
        mine = gath[it].at[core, hz, q]
        return remote(mine, mine, side_s.at[it, m - 1], side_r.at[it, m - 1], *on_side(m))

    def relay(it, k, m):
        got = gath[it].at[core, lax.rem(hz - k + nz, nz), q]
        return remote(
            got, got, pass_s.at[it, k - 1, m - 1], pass_r.at[it, k - 1, m - 1], *on_side(m)
        )

    def mate(it, k):
        plane = gath[it].at[core, lax.rem(hz - k + nz, nz)]
        return remote(plane, plane, mate_s.at[it, k], mate_r.at[it, k], partner, me_x)

    def gather_begin(it):
        for k in range(1, nz):
            line(it, k).start()
        for m in range(1, nq):
            side(it, m).start()

    def gather_relay(it):
        for k in range(1, nz):
            line(it, k).wait()
            for m in range(1, nq):
                relay(it, k, m).start()

    def gather_mate(it):
        for m in range(1, nq):
            side(it, m).wait()
        mate(it, 0).start()

    def gather_end(it):
        for k in range(1, nz):
            for m in range(1, nq):
                relay(it, k, m).wait()
            mate(it, k).start()
        for k in range(nz):
            mate(it, k).wait()

    def coeffs(it):
        acc = jnp.zeros((2 * cols, 2 * bs), F32)
        for t in range(nb2):
            x = jnp.concatenate([ur[2 * t], ur[2 * t + 1]], axis=1)
            acc = acc + dot_nn(x, bt[t])
        gath[it][core, hz, q] = fold(acc)

    def pick(u, b):
        return jnp.concatenate([u[b], u[oidx[0, b]], u[oidx[1, b]]], axis=1)

    def row(u, b):
        return fold(dot_nn(pick(u, b), w[b]))

    BATCH = 5

    def middle(u, emit, lo=1, hi=None):
        hi = nb - 1 if hi is None else hi
        for first in range(lo, hi, BATCH):
            rows = list(range(first, min(first + BATCH, hi)))
            emit(rows, [row(u, b) for b in rows])

    def first_last(u):
        y0 = row(u, 0) + fold(dot_nn(u[left], wc[0]))
        y1 = row(u, nb - 1) + fold(dot_nn(u[right], wc[1]))
        return y0, y1

    def outer(u):
        yl = fold(dot_nn(jnp.concatenate([u[left], u[0]], axis=1), wt[0]))
        yr = fold(dot_nn(jnp.concatenate([u[right], u[nb - 1]], axis=1), wt[1]))
        return yl, yr

    coefs = cheb_coefs()

    def emit_step(k, unew):
        ca, cc = coefs[k]

        def emit(rows, ys):
            out = []
            for b, y in zip(rows, ys):
                rv = r[b]
                if k == 0:
                    dv = rv * (1.0 / THETA)
                    zv = dv
                    y = y * (1.0 / THETA)
                else:
                    dv = d[b]
                    zv = z[b]
                dv = ca * dv + cc * (rv - y)
                out.append((dv, zv + dv))
            for b, (dv, zv) in zip(rows, out):
                if k + 2 < ORDER:
                    d[b] = dv
                    put(unew, b, zv)
                z[b] = zv

        return emit

    def ends_step(k, u, unew):
        yl, yr = outer(u)
        y0, y1 = first_last(u)
        emit_step(k, unew)([0, nb - 1, left, right], [y0, y1, yl, yr])

    def outer_operator():
        wait_both(op_copies)
        for side in range(2):
            for j in range(2):
                hi, lo = halves(op_in[side, j])
                wt[side, j * bs : (j + 1) * bs, 0:bs] = hi.T
                wt[side, j * bs : (j + 1) * bs, bs : 2 * bs] = lo.T

    def out_copy(i, b):
        return pltpu.make_async_copy((sv, r)[i].at[b], (sol, res)[i].at[:, b], osem.at[i, b])

    def iteration(it):
        last = it + 1 == ITERS
        if it > 0:
            middle(ur, emit_step(0, ua))
        wait_both(functools.partial(r_copy, it))
        for side, b in ((0, left), (1, right)):
            v = r_in[it, side]
            r[b] = v
            put(ur, b, v)
        ends_step(0, ur, ua)
        ends_step(1, ua, ub)
        middle(ua, emit_step(1, ub))
        half = nb // 2
        ends_step(2, ub, ua)
        middle(ub, emit_step(2, ua), 1, half)
        gather_relay(it)
        middle(ub, emit_step(2, ua), half, nb - 1)
        gather_mate(it)
        ends_step(3, ua, ub)
        middle(ua, emit_step(3, ub))
        gather_end(it)

        xs = []
        for j in range(ncb):
            g = cidx[j]
            s = g // nc
            hi, lo = halves(
                gath[it][
                    lax.rem(s, 2), s // 2 // ny, lax.rem(s // 2, ny) * nc + lax.rem(g, nc)
                ]
            )
            xs.append(jnp.concatenate([hi, lo], axis=0))
        csol = fold(dot_nn(jnp.concatenate(xs, axis=1), cw[...]))
        hi, lo = halves(csol)
        cx = jnp.concatenate([hi, lo], axis=0)
        cx = jnp.concatenate([cx, cx], axis=1)

        def spread(t):
            o = dot_nn(cx, bw[t])
            o = o[:cols] + o[cols:]
            return o[:, :bs], o[:, bs:]

        def keep(b, v):
            sv[b] = v if it == 0 else sv[b] + v
            put(ub, b, v)

        a0, a1 = spread(0)
        b0, b1 = spread(nb2 - 1)
        edge_l = z[0] + a0
        edge_r = z[nb - 1] + b1
        e_out[it, 1, 0] = z[left]
        e_out[it, 1, 1] = edge_l
        e_out[it, 0, 0] = z[right]
        e_out[it, 0, 1] = edge_r
        start_both(functools.partial(e_copy, it))
        keep(1, z[1] + a1)
        keep(nb - 2, z[nb - 2] + b0)
        for t in range(1, nb2 - 1):
            v0, v1 = spread(t)
            keep(2 * t, z[2 * t] + v0)
            keep(2 * t + 1, z[2 * t + 1] + v1)
        if last:
            for b in range(1, nb - 1):
                out_copy(0, b).start()
        wait_both(functools.partial(e_copy, it))
        keep(0, edge_l + e_in[it, 0, 0])
        keep(nb - 1, edge_r + e_in[it, 1, 0])
        put(ub, left, e_in[it, 0, 1] + z[left])
        put(ub, right, e_in[it, 1, 1] + z[right])
        if last:
            for b in (0, nb - 1):
                out_copy(0, b).start()

        def emit_res(rows, ys):
            vals = [r[b] - y for b, y in zip(rows, ys)]
            for b, v in zip(rows, vals):
                r[b] = v
                if not last:
                    put(ur, b, v)

        emit_res([0, nb - 1], list(first_last(ub)))
        if not last:
            start_both(functools.partial(r_copy, it + 1))
            middle(ub, emit_res)
            coeffs(it + 1)
            gather_begin(it + 1)
        else:
            for b in (0, nb - 1):
                out_copy(1, b).start()
            for first in range(1, nb - 1, 2 * BATCH):
                end = min(first + 2 * BATCH, nb - 1)
                middle(ub, emit_res, first, end)
                for b in range(first, end):
                    out_copy(1, b).start()
            for i in range(2):
                for b in range(nb):
                    out_copy(i, b).wait()

    coeffs(0)
    gather_begin(0)
    ld[2].wait()
    for j in range(2):
        hi, lo = halves(f_couple[j])
        wc[j, :, 0:bs] = hi.T
        wc[j, :, bs : 2 * bs] = lo.T
    outer_operator()

    step0 = emit_step(0, ua)
    for c in range(CHUNKS):
        for copy in ldw[c]:
            copy.wait()
        rows, ys = [], []
        for b in range(c * chunk, (c + 1) * chunk):
            parts = []
            for v in (f_diag[b], f_offs[b, 0], f_offs[b, 1]):
                hi, lo = halves(v)
                parts.append(jnp.concatenate([hi.T, lo.T], axis=1))
            wv = jnp.concatenate(parts, axis=0)
            w[b] = wv
            if 0 < b < nb - 1:
                rows.append(b)
                ys.append(fold(dot_nn(pick(ur, b), wv)))
            if len(rows) == 4 or b == (c + 1) * chunk - 1:
                step0(rows, ys)
                rows, ys = [], []
    ld[3].wait()
    for j in range(ncb):
        hi, lo = halves(f_cblk[j])
        cw[j * bs : (j + 1) * bs, 0:bs] = hi.T
        cw[j * bs : (j + 1) * bs, bs : 2 * bs] = lo.T
    for it in range(ITERS):
        iteration(it)


def per_device(ns, nc, loads, diag, offs, oidx, couple, basis, cblk, cidx):
    _, cols, nb, bs = loads.shape
    k = basis.shape[1]
    ncb = cblk.shape[1]
    ny = 2 if ns % 4 == 0 else 1
    nz = ns // 2 // ny
    nq = ny * nc
    anyspace = pl.BlockSpec(memory_space=pl.ANY)
    smem = pl.BlockSpec(memory_space=pltpu.SMEM)
    field = (nb + 2, cols, bs)
    ufield = (nb + 2, 2 * cols, bs)
    dma = pltpu.SemaphoreType.DMA
    out = jax.ShapeDtypeStruct((cols, nb, bs), F32)
    sol, res = pl.pallas_call(
        functools.partial(kernel, ns, nc, ny, nb, cols, bs, ncb),
        out_shape=(out, out),
        in_specs=[anyspace, anyspace, anyspace, smem, anyspace, anyspace, anyspace, smem],
        out_specs=(anyspace, anyspace),
        scratch_shapes=[
            pltpu.VMEM((cols * nb, bs), F32),
            pltpu.VMEM((nb, bs, bs), F32),
            pltpu.VMEM((nb, 2, bs, bs), F32),
            pltpu.VMEM((2, bs, bs), F32),
            pltpu.VMEM((k * nb, bs), F32),
            pltpu.VMEM((ncb, bs, bs), F32),
            pltpu.VMEM((nb, 3 * bs, 2 * bs), BF16),
            pltpu.VMEM((2, bs, 2 * bs), BF16),
            pltpu.VMEM((2, 2 * bs, 2 * bs), BF16),
            pltpu.VMEM((nb // 2, 2 * bs, 2 * bs), BF16),
            pltpu.VMEM((nb // 2, 2 * bs, 2 * bs), BF16),
            pltpu.VMEM((ncb * bs, 2 * bs), BF16),
            pltpu.VMEM(field, F32),
            pltpu.VMEM(field, F32),
            pltpu.VMEM(field, F32),
            pltpu.VMEM((nb, cols, bs), F32),
            pltpu.VMEM(ufield, BF16),
            pltpu.VMEM(ufield, BF16),
            pltpu.VMEM(ufield, BF16),
            pltpu.VMEM((2, nz, nq, cols, bs), F32),
            pltpu.VMEM((2, nz, nq, cols, bs), F32),
            pltpu.VMEM((2, 2, bs, bs), F32),
            pltpu.VMEM((ITERS, 2, cols, bs), F32),
            pltpu.VMEM((ITERS, 2, 2, cols, bs), F32),
            pltpu.VMEM((ITERS, 2, 2, cols, bs), F32),
            dma((4,)),
            dma((2, CHUNKS)),
            dma((2, nb)),
            dma((2, 2)),
            dma((2, 2)),
            dma((ITERS, 2)),
            dma((ITERS, 2)),
            dma((ITERS, 2)),
            dma((ITERS, 2)),
            dma((ITERS, max(nz - 1, 1))),
            dma((ITERS, max(nz - 1, 1))),
            dma((ITERS, max(nq - 1, 1))),
            dma((ITERS, max(nq - 1, 1))),
            dma((ITERS, max(nz - 1, 1), max(nq - 1, 1))),
            dma((ITERS, max(nz - 1, 1), max(nq - 1, 1))),
            dma((ITERS, nz)),
            dma((ITERS, nz)),
        ],
        compiler_params=pltpu.CompilerParams(
            collective_id=0, has_side_effects=True, vmem_limit_bytes=56 * 1024 * 1024
        ),
    )(
        loads.reshape(cols * nb, bs), diag[0], offs[0], oidx[0].T, couple[0],
        basis.reshape(k * nb, bs), cblk[0], cidx[0],
    )
    return sol[None], res[None]


def solution(mesh):
    lead = ("sub", "coarse")
    in_specs = (
        P(lead, None, None, None),
        P(lead, None, None, None),
        P(lead, None, None, None, None),
        P(lead, None, None),
        P(lead, None, None, None),
        P(lead, None, None, None),
        P(lead, None, None, None),
        P(lead, None),
    )
    out_specs = (P(lead, None, None, None), P(lead, None, None, None))
    return jax.shard_map(
        functools.partial(per_device, mesh.shape["sub"], mesh.shape["coarse"]),
        mesh=mesh, in_specs=in_specs, out_specs=out_specs, check_vma=False,
    )
```

```python
import functools

import jax
import jax.numpy as jnp
from jax import lax
from jax.experimental import pallas as pl
from jax.experimental.pallas import tpu as pltpu
from jax.sharding import PartitionSpec as P

ORDER = 5
ITERS = 2
THETA = 5.0
DELTA = 4.0
F32 = jnp.float32
BF16 = jnp.bfloat16
MESH = pl.DeviceIdType.MESH
CHUNKS = 4
BGROUP = 4


def cheb_coefs():
    sigma = THETA / DELTA
    rho = 1.0 / sigma
    out = []
    for _ in range(ORDER - 1):
        nxt = 1.0 / (2.0 * sigma - rho)
        out.append((nxt * rho, 2.0 * nxt / DELTA))
        rho = nxt
    return out


def halves(v):
    hi = v.astype(BF16)
    lo = (v - hi.astype(F32)).astype(BF16)
    return hi, lo


def dot_nt(x, w):
    return lax.dot_general(x, w, (((1,), (1,)), ((), ())), preferred_element_type=F32)


def dot_nn(x, w):
    return lax.dot_general(x, w, (((1,), (0,)), ((), ())), preferred_element_type=F32)


def kernel(
    ns, nc, nb, cols, bs, ncb,
    loads, diag, offs, oidx_any, couple, basis, cblk, cidx_any,
    first_sum, second_sum,
    oidx, cidx,
    f_loads, f_diag, f_offs, f_couple, f_basis, f_cblk,
    w, wc, wt, bw, bt, cw,
    r, d, z, ua, ub, ur,
    gath0, gath1, op_in, r_in, e_in, e_out,
    lsem, wsem, op_s, op_r, rh_s, rh_r, e_s, e_r, all_s, all_r, mate_s, mate_r,
):
    me_s = lax.axis_index("sub")
    me_x = lax.axis_index("coarse")
    core = lax.rem(me_s, 2)
    h = me_s // 2
    peers = ns // 2 * nc
    own = h * nc + me_x
    partner = me_s + 1 - 2 * core
    has_l = me_s > 0
    has_r = me_s < ns - 1
    nb2 = nb // 2
    left, right = nb, nb + 1
    chunk = nb // CHUNKS

    ld = [
        pltpu.make_async_copy(loads, f_loads, lsem.at[0]),
        pltpu.make_async_copy(basis, f_basis, lsem.at[1]),
        pltpu.make_async_copy(couple, f_couple, lsem.at[2]),
        pltpu.make_async_copy(cblk, f_cblk, lsem.at[3]),
        pltpu.make_async_copy(oidx_any, oidx, lsem.at[4]),
        pltpu.make_async_copy(cidx_any, cidx, lsem.at[5]),
    ]
    ldw = [
        [
            pltpu.make_async_copy(src.at[span], dst.at[span], wsem.at[c])
            for src, dst in ((diag, f_diag), (offs, f_offs))
        ]
        for c, span in enumerate(pl.ds(c * chunk, chunk) for c in range(CHUNKS))
    ]
    for c in (ld[0], ld[1], ld[4], ld[5], ld[2]):
        c.start()
    for pair in ldw:
        for c in pair:
            c.start()
    ld[3].start()

    def remote(src, dst, ss, rs, s, x):
        return pltpu.make_async_remote_copy(
            src_ref=src, dst_ref=dst, send_sem=ss, recv_sem=rs,
            device_id={"sub": s, "coarse": x}, device_id_type=MESH,
        )

    barrier = pltpu.get_barrier_semaphore()

    def greet(s, x):
        pl.semaphore_signal(
            barrier, inc=1, device_id={"sub": s, "coarse": x}, device_id_type=MESH
        )

    def peer(k):
        to = lax.rem(own + k, peers)
        return core + 2 * (to // nc), lax.rem(to, nc)

    for k in range(1, peers):
        greet(*peer(k))

    @pl.when(has_l)
    def _():
        greet(me_s - 1, me_x)

    @pl.when(has_r)
    def _():
        greet(me_s + 1, me_x)

    for side, has in ((0, has_l), (1, has_r)):

        @pl.when(jnp.logical_not(has))
        def _():
            op_in[side] = jnp.zeros_like(op_in[side])
            for it in range(ITERS):
                r_in[it, side] = jnp.zeros_like(r_in[it, side])
                e_in[it, side] = jnp.zeros_like(e_in[it, side])

    def put(ref, b, v):
        hi, lo = halves(v)
        ref[b, 0:cols, :] = hi
        ref[b, cols : 2 * cols, :] = lo

    def fold(o):
        return (o[:cols, :bs] + o[:cols, bs:]) + (o[cols:, :bs] + o[cols:, bs:])

    ld[0].wait()

    for b in range(nb):
        v = f_loads[pl.ds(b, cols, stride=nb), :]
        r[b] = v
        put(ur, b, v)
    pl.semaphore_wait(
        barrier, peers - 1 + has_l.astype(jnp.int32) + has_r.astype(jnp.int32)
    )

    def op_copies(to_left):
        b = 0 if to_left else nb - 1
        side = 1 if to_left else 0
        s = me_s - 1 if to_left else me_s + 1
        return [
            remote(diag.at[b], op_in.at[side, 0], op_s.at[side], op_r.at[side], s, me_x),
            remote(
                couple.at[0 if to_left else 1], op_in.at[side, 1],
                op_s.at[side], op_r.at[side], s, me_x,
            ),
        ]

    def op_both(to_left):
        side = 1 if to_left else 0
        s = me_s - 1 if to_left else me_s + 1
        return [remote(op_in.at[side], op_in.at[side], op_s.at[side], op_r.at[side], s, me_x)]

    def r_copy(it, to_left):
        b = 0 if to_left else nb - 1
        side = 1 if to_left else 0
        s = me_s - 1 if to_left else me_s + 1
        return [remote(r.at[b], r_in.at[it, side], rh_s.at[it, side], rh_r.at[it, side], s, me_x)]

    def e_copy(it, to_left):
        side = 1 if to_left else 0
        s = me_s - 1 if to_left else me_s + 1
        return [
            remote(
                e_out.at[it, side], e_in.at[it, side], e_s.at[it, side], e_r.at[it, side], s, me_x
            )
        ]

    def start_both(make):
        @pl.when(has_l)
        def _():
            for c in make(True):
                c.start()

        @pl.when(has_r)
        def _():
            for c in make(False):
                c.start()

    def wait_both(make):
        @pl.when(has_l)
        def _():
            for c in make(True):
                c.wait_send()
            for c in make(False):
                c.wait_recv()

        @pl.when(has_r)
        def _():
            for c in make(False):
                c.wait_send()
            for c in make(True):
                c.wait_recv()

    start_both(functools.partial(r_copy, 0))
    start_both(op_copies)
    ld[1].wait()

    def init_basis(g, carry):
        for p in range(BGROUP):
            t = g * BGROUP + p
            for e in range(2):
                hi, lo = halves(f_basis[pl.ds(2 * t + e, bs, stride=nb), :])
                cut = slice(e * bs, (e + 1) * bs)
                bw[t, 0:bs, cut] = hi
                bw[t, bs : 2 * bs, cut] = lo
                bt[t, cut, 0:bs] = hi.T
                bt[t, cut, bs : 2 * bs] = lo.T
        return carry

    lax.fori_loop(0, nb2 // BGROUP, init_basis, 0)

    gath = (gath0, gath1)

    def gather_begin(it):
        for k in sorted(range(1, peers), key=lambda k: abs(2 * k - peers)):
            mine = gath[it].at[core, own]
            remote(mine, mine, all_s.at[it], all_r.at[it], *peer(k)).start()

    def mate(it):
        mine = gath[it].at[core]
        return remote(mine, mine, mate_s.at[it], mate_r.at[it], partner, me_x)

    def gather_end(it):
        rest = gath[it].at[core, pl.ds(0, peers - 1)]
        remote(rest, rest, all_s.at[it], all_r.at[it], *peer(1)).wait()
        mate(it).start()
        mate(it).wait()

    def coeffs(it):
        acc = jnp.zeros((2 * cols, 2 * bs), F32)
        for t in range(nb2):
            x = jnp.concatenate([ur[2 * t], ur[2 * t + 1]], axis=1)
            acc = acc + dot_nn(x, bt[t])
        gath[it][core, own] = fold(acc)

    def pick(u, b):
        return jnp.concatenate([u[b], u[oidx[0, b]], u[oidx[1, b]]], axis=1)

    def row(u, b):
        return fold(dot_nn(pick(u, b), w[b]))

    BATCH = 5

    def middle(u, emit, lo=1, hi=None):
        hi = nb - 1 if hi is None else hi
        for first in range(lo, hi, BATCH):
            rows = list(range(first, min(first + BATCH, hi)))
            emit(rows, [row(u, b) for b in rows])

    def first_last(u):
        y0 = row(u, 0) + fold(dot_nn(u[left], wc[0]))
        y1 = row(u, nb - 1) + fold(dot_nn(u[right], wc[1]))
        return y0, y1

    def outer(u):
        yl = fold(dot_nn(jnp.concatenate([u[left], u[0]], axis=1), wt[0]))
        yr = fold(dot_nn(jnp.concatenate([u[right], u[nb - 1]], axis=1), wt[1]))
        return yl, yr

    coefs = cheb_coefs()

    def emit_step(k, unew):
        ca, cc = coefs[k]

        def emit(rows, ys):
            out = []
            for b, y in zip(rows, ys):
                rv = r[b]
                if k == 0:
                    dv = rv * (1.0 / THETA)
                    zv = dv
                    y = y * (1.0 / THETA)
                else:
                    dv = d[b]
                    zv = z[b]
                dv = ca * dv + cc * (rv - y)
                out.append((dv, zv + dv))
            for b, (dv, zv) in zip(rows, out):
                if k + 2 < ORDER:
                    d[b] = dv
                    put(unew, b, zv)
                z[b] = zv

        return emit

    def ends_step(k, u, unew):
        yl, yr = outer(u)
        y0, y1 = first_last(u)
        emit_step(k, unew)([0, nb - 1, left, right], [y0, y1, yl, yr])

    def outer_operator():
        wait_both(op_both)
        for side in range(2):
            for j in range(2):
                hi, lo = halves(op_in[side, j])
                wt[side, j * bs : (j + 1) * bs, 0:bs] = hi.T
                wt[side, j * bs : (j + 1) * bs, bs : 2 * bs] = lo.T

    def iteration(it):
        last = it + 1 == ITERS
        if it > 0:
            middle(ur, emit_step(0, ua))
        wait_both(functools.partial(r_copy, it))
        for side, b in ((0, left), (1, right)):
            v = r_in[it, side]
            r[b] = v
            put(ur, b, v)
        ends_step(0, ur, ua)
        ends_step(1, ua, ub)
        middle(ua, emit_step(1, ub))
        ends_step(2, ub, ua)
        middle(ub, emit_step(2, ua))
        ends_step(3, ua, ub)
        middle(ua, emit_step(3, ub))
        gather_end(it)

        xs = []
        for j in range(ncb):
            g = cidx[j]
            s = g // nc
            hi, lo = halves(
                gath[it][lax.rem(s, 2), s // 2 * nc + lax.rem(g, nc)]
            )
            xs.append(jnp.concatenate([hi, lo], axis=0))
        csol = fold(dot_nn(jnp.concatenate(xs, axis=1), cw[...]))
        hi, lo = halves(csol)
        cx = jnp.concatenate([hi, lo], axis=0)
        cx = jnp.concatenate([cx, cx], axis=1)

        def spread(t):
            o = dot_nn(cx, bw[t])
            o = o[:cols] + o[cols:]
            return o[:, :bs], o[:, bs:]

        def keep(b, v):
            (second_sum if last else first_sum)[0, pl.ds(b, cols, stride=nb), :] = v
            put(ub, b, v)

        a0, a1 = spread(0)
        b0, b1 = spread(nb2 - 1)
        edge_l = z[0] + a0
        edge_r = z[nb - 1] + b1
        e_out[it, 1, 0] = z[left]
        e_out[it, 1, 1] = edge_l
        e_out[it, 0, 0] = z[right]
        e_out[it, 0, 1] = edge_r
        start_both(functools.partial(e_copy, it))
        keep(1, z[1] + a1)
        keep(nb - 2, z[nb - 2] + b0)
        for t in range(1, nb2 - 1):
            v0, v1 = spread(t)
            keep(2 * t, z[2 * t] + v0)
            keep(2 * t + 1, z[2 * t + 1] + v1)
        wait_both(functools.partial(e_copy, it))
        keep(0, edge_l + e_in[it, 0, 0])
        keep(nb - 1, edge_r + e_in[it, 1, 0])
        put(ub, left, e_in[it, 0, 1] + z[left])
        put(ub, right, e_in[it, 1, 1] + z[right])

        def emit_res(rows, ys):
            if last:
                for b, y in zip(rows, ys):
                    second_sum[1, pl.ds(b, cols, stride=nb), :] = -y
                return
            vals = [r[b] - y for b, y in zip(rows, ys)]
            for b, v in zip(rows, vals):
                r[b] = v
                first_sum[1, pl.ds(b, cols, stride=nb), :] = v
                put(ur, b, v)

        emit_res([0, nb - 1], list(first_last(ub)))
        if not last:
            start_both(functools.partial(r_copy, it + 1))
        middle(ub, emit_res)
        if not last:
            coeffs(it + 1)
            gather_begin(it + 1)

    coeffs(0)
    gather_begin(0)
    ld[2].wait()
    for j in range(2):
        hi, lo = halves(f_couple[j])
        wc[j, :, 0:bs] = hi.T
        wc[j, :, bs : 2 * bs] = lo.T

    ld[4].wait()
    ld[5].wait()
    step0 = emit_step(0, ua)
    for c in range(CHUNKS):
        both = pl.ds(0, 3 * chunk)
        pltpu.make_async_copy(diag.at[both], f_diag.at[both], wsem.at[c]).wait()
        rows, ys = [], []
        for b in range(c * chunk, (c + 1) * chunk):
            parts = []
            for v in (f_diag[b], f_offs[b, 0], f_offs[b, 1]):
                hi, lo = halves(v)
                parts.append(jnp.concatenate([hi.T, lo.T], axis=1))
            wv = jnp.concatenate(parts, axis=0)
            w[b] = wv
            if 0 < b < nb - 1:
                rows.append(b)
                ys.append(fold(dot_nn(pick(ur, b), wv)))
            if len(rows) == 4 or b == (c + 1) * chunk - 1:
                step0(rows, ys)
                rows, ys = [], []
    outer_operator()
    ld[3].wait()
    for j in range(ncb):
        hi, lo = halves(f_cblk[j])
        cw[j * bs : (j + 1) * bs, 0:bs] = hi.T
        cw[j * bs : (j + 1) * bs, bs : 2 * bs] = lo.T
    for it in range(ITERS):
        iteration(it)


def per_device(ns, nc, loads, diag, offs, oidx, couple, basis, cblk, cidx):
    _, cols, nb, bs = loads.shape
    k = basis.shape[1]
    ncb = cblk.shape[1]
    peers = ns // 2 * nc
    anyspace = pl.BlockSpec(memory_space=pl.ANY)
    vmem = pl.BlockSpec(memory_space=pltpu.VMEM)
    field = (nb + 2, cols, bs)
    ufield = (nb + 2, 2 * cols, bs)
    dma = pltpu.SemaphoreType.DMA
    out = pltpu.VMEM((2, cols * nb, bs), F32)
    first, second = pl.pallas_call(
        functools.partial(kernel, ns, nc, nb, cols, bs, ncb),
        out_shape=(out, out),
        in_specs=[anyspace] * 8,
        out_specs=(vmem, vmem),
        scratch_shapes=[
            pltpu.SMEM((2, nb), jnp.int32),
            pltpu.SMEM((ncb,), jnp.int32),
            pltpu.VMEM((cols * nb, bs), F32),
            pltpu.VMEM((nb, bs, bs), F32),
            pltpu.VMEM((nb, 2, bs, bs), F32),
            pltpu.VMEM((2, bs, bs), F32),
            pltpu.VMEM((k * nb, bs), F32),
            pltpu.VMEM((ncb, bs, bs), F32),
            pltpu.VMEM((nb, 3 * bs, 2 * bs), BF16),
            pltpu.VMEM((2, bs, 2 * bs), BF16),
            pltpu.VMEM((2, 2 * bs, 2 * bs), BF16),
            pltpu.VMEM((nb // 2, 2 * bs, 2 * bs), BF16),
            pltpu.VMEM((nb // 2, 2 * bs, 2 * bs), BF16),
            pltpu.VMEM((ncb * bs, 2 * bs), BF16),
            pltpu.VMEM(field, F32),
            pltpu.VMEM(field, F32),
            pltpu.VMEM(field, F32),
            pltpu.VMEM(ufield, BF16),
            pltpu.VMEM(ufield, BF16),
            pltpu.VMEM(ufield, BF16),
            pltpu.VMEM((2, peers, cols, bs), F32),
            pltpu.VMEM((2, peers, cols, bs), F32),
            pltpu.VMEM((2, 2, bs, bs), F32),
            pltpu.VMEM((ITERS, 2, cols, bs), F32),
            pltpu.VMEM((ITERS, 2, 2, cols, bs), F32),
            pltpu.VMEM((ITERS, 2, 2, cols, bs), F32),
            dma((6,)),
            dma((CHUNKS,)),
            dma((2,)),
            dma((2,)),
            dma((ITERS, 2)),
            dma((ITERS, 2)),
            dma((ITERS, 2)),
            dma((ITERS, 2)),
            dma((ITERS,)),
            dma((ITERS,)),
            dma((ITERS,)),
            dma((ITERS,)),
        ],
        compiler_params=pltpu.CompilerParams(
            collective_id=0, has_side_effects=True, vmem_limit_bytes=56 * 1024 * 1024
        ),
    )(
        loads.reshape(cols * nb, bs), diag[0], offs[0], oidx[0].T, couple[0],
        basis.reshape(k * nb, bs), cblk[0], cidx[0],
    )
    total = first + second
    shape = (1, cols, nb, bs)
    return total[0].reshape(shape), total[1].reshape(shape)


def solution(mesh):
    lead = ("sub", "coarse")
    in_specs = (
        P(lead, None, None, None),
        P(lead, None, None, None),
        P(lead, None, None, None, None),
        P(lead, None, None),
        P(lead, None, None, None),
        P(lead, None, None, None),
        P(lead, None, None, None),
        P(lead, None),
    )
    out_specs = (P(lead, None, None, None), P(lead, None, None, None))
    return jax.shard_map(
        functools.partial(per_device, mesh.shape["sub"], mesh.shape["coarse"]),
        mesh=mesh, in_specs=in_specs, out_specs=out_specs, check_vma=False,
    )
```

```python
import functools

import jax
import jax.numpy as jnp
from jax import lax
from jax.experimental import pallas as pl
from jax.experimental.pallas import tpu as pltpu
from jax.sharding import PartitionSpec as P

ORDER = 5
ITERS = 2
THETA = 5.0
DELTA = 4.0
F32 = jnp.float32
BF16 = jnp.bfloat16
MESH = pl.DeviceIdType.MESH
CHUNKS = 4


def cheb_coefs():
    sigma = THETA / DELTA
    rho = 1.0 / sigma
    out = []
    for _ in range(ORDER - 1):
        nxt = 1.0 / (2.0 * sigma - rho)
        out.append((nxt * rho, 2.0 * nxt / DELTA))
        rho = nxt
    return out


def hops(n):
    return sorted(range(1, n), key=lambda k: min(k, n - k))


def halves(v):
    hi = v.astype(BF16)
    lo = (v - hi.astype(F32)).astype(BF16)
    return hi, lo


def dot_nt(x, w):
    return lax.dot_general(x, w, (((1,), (1,)), ((), ())), preferred_element_type=F32)


def dot_nn(x, w):
    return lax.dot_general(x, w, (((1,), (0,)), ((), ())), preferred_element_type=F32)


def kernel(
    ns, nc, ny, nb, cols, bs, ncb,
    loads, diag, offs, oidx_any, couple, basis, cblk, cidx_any,
    first_sum, second_sum,
    oidx, cidx,
    f_loads, f_diag, f_offs, f_couple, f_basis, f_cblk,
    w, wc, wt, bw, cw,
    r, d, z, ua, ub, ur,
    gath0, gath1, op_in, r_in, e_in, e_out, a_in, a_out,
    lsem, wsem, op_s, op_r, rh_s, rh_r, e_s, e_r, a_s, a_r,
    line_s, line_r, side_s, side_r, pass_s, pass_r, mate_s, mate_r,
):
    me_s = lax.axis_index("sub")
    me_x = lax.axis_index("coarse")
    core = lax.rem(me_s, 2)
    h = me_s // 2
    nz = ns // 2 // ny
    nq = ny * nc
    hz = h // ny
    q = lax.rem(h, ny) * nc + me_x
    partner = me_s + 1 - 2 * core
    has_l = me_s > 0
    has_r = me_s < ns - 1
    nb2 = nb // 2
    left, right = nb, nb + 1
    chunk = nb // CHUNKS

    ld = [
        pltpu.make_async_copy(loads, f_loads, lsem.at[0]),
        pltpu.make_async_copy(basis, f_basis, lsem.at[1]),
        pltpu.make_async_copy(couple, f_couple, lsem.at[2]),
        pltpu.make_async_copy(cblk, f_cblk, lsem.at[3]),
        pltpu.make_async_copy(oidx_any, oidx, lsem.at[4]),
        pltpu.make_async_copy(cidx_any, cidx, lsem.at[5]),
    ]
    ldw = [
        [
            pltpu.make_async_copy(src.at[span], dst.at[span], wsem.at[c])
            for src, dst in ((diag, f_diag), (offs, f_offs))
        ]
        for c, span in enumerate(pl.ds(c * chunk, chunk) for c in range(CHUNKS))
    ]
    for c in (ld[0], ld[1], ld[4], ld[5], ld[2]):
        c.start()

    def remote(src, dst, ss, rs, s, x):
        return pltpu.make_async_remote_copy(
            src_ref=src, dst_ref=dst, send_sem=ss, recv_sem=rs,
            device_id={"sub": s, "coarse": x}, device_id_type=MESH,
        )

    barrier = pltpu.get_barrier_semaphore()

    def greet(s, x):
        pl.semaphore_signal(
            barrier, inc=1, device_id={"sub": s, "coarse": x}, device_id_type=MESH
        )

    def on_line(k):
        return core + 2 * (lax.rem(hz + k, nz) * ny + lax.rem(h, ny)), me_x

    def on_side(m):
        to = lax.rem(q + m, nq)
        return core + 2 * (hz * ny + to // nc), lax.rem(to, nc)

    for k in range(1, nz):
        greet(*on_line(k))
    for m in range(1, nq):
        greet(*on_side(m))

    @pl.when(has_l)
    def _():
        greet(me_s - 1, me_x)

    @pl.when(has_r)
    def _():
        greet(me_s + 1, me_x)

    for side, has in ((0, has_l), (1, has_r)):

        @pl.when(jnp.logical_not(has))
        def _():
            op_in[side] = jnp.zeros_like(op_in[side])
            for it in range(ITERS):
                r_in[it, side] = jnp.zeros_like(r_in[it, side])
                e_in[it, side] = jnp.zeros_like(e_in[it, side])
                a_in[it, side] = jnp.zeros_like(a_in[it, side])

    def put(ref, b, v):
        hi, lo = halves(v)
        ref[b, 0:cols, :] = hi
        ref[b, cols : 2 * cols, :] = lo

    def fold(o):
        return (o[:cols, :bs] + o[:cols, bs:]) + (o[cols:, :bs] + o[cols:, bs:])

    ld[0].wait()

    for b in range(nb):
        v = f_loads[pl.ds(b, cols, stride=nb), :]
        r[b] = v
        put(ur, b, v)
    for pair in ldw:
        for c in pair:
            c.start()
    ld[3].start()
    pl.semaphore_wait(
        barrier, nz - 1 + nq - 1 + has_l.astype(jnp.int32) + has_r.astype(jnp.int32)
    )

    def op_copies(to_left):
        b = 0 if to_left else nb - 1
        side = 1 if to_left else 0
        s = me_s - 1 if to_left else me_s + 1
        return [
            remote(diag.at[b], op_in.at[side, 0], op_s.at[side], op_r.at[side], s, me_x),
            remote(
                couple.at[0 if to_left else 1], op_in.at[side, 1],
                op_s.at[side], op_r.at[side], s, me_x,
            ),
        ]

    def op_both(to_left):
        side = 1 if to_left else 0
        s = me_s - 1 if to_left else me_s + 1
        return [remote(op_in.at[side], op_in.at[side], op_s.at[side], op_r.at[side], s, me_x)]

    def r_copy(it, to_left):
        b = 0 if to_left else nb - 1
        side = 1 if to_left else 0
        s = me_s - 1 if to_left else me_s + 1
        return [remote(r.at[b], r_in.at[it, side], rh_s.at[it, side], rh_r.at[it, side], s, me_x)]

    def e_copy(it, to_left):
        side = 1 if to_left else 0
        s = me_s - 1 if to_left else me_s + 1
        return [
            remote(
                e_out.at[it, side], e_in.at[it, side], e_s.at[it, side], e_r.at[it, side], s, me_x
            )
        ]

    def a_copy(it, to_left):
        side = 1 if to_left else 0
        s = me_s - 1 if to_left else me_s + 1
        return [
            remote(
                a_out.at[it, side], a_in.at[it, side], a_s.at[it, side], a_r.at[it, side], s, me_x
            )
        ]

    def start_both(make):
        @pl.when(has_l)
        def _():
            for c in make(True):
                c.start()

        @pl.when(has_r)
        def _():
            for c in make(False):
                c.start()

    def wait_both(make):
        @pl.when(has_l)
        def _():
            for c in make(True):
                c.wait_send()
            for c in make(False):
                c.wait_recv()

        @pl.when(has_r)
        def _():
            for c in make(False):
                c.wait_send()
            for c in make(True):
                c.wait_recv()

    start_both(functools.partial(r_copy, 0))
    start_both(op_copies)
    ld[1].wait()

    gath = (gath0, gath1)

    def plane(it, k):
        return gath[it].at[core, lax.rem(hz - k + nz, nz)]

    def line(it, k):
        mine = gath[it].at[core, hz, q]
        return remote(mine, mine, line_s.at[it, k - 1], line_r.at[it, k - 1], *on_line(k))

    def mate(it, k):
        return remote(plane(it, k), plane(it, k), mate_s.at[it], mate_r.at[it], partner, me_x)

    def gather_begin(it):
        for k in hops(nz):
            line(it, k).start()
        mine = gath[it].at[core, hz, q]
        for m in range(1, nq):
            remote(mine, mine, side_s.at[it], side_r.at[it], *on_side(m)).start()

    def gather_relay(it):
        for k in hops(nz):
            line(it, k).wait()
            got = plane(it, k).at[q]
            for m in range(1, nq):
                remote(
                    got, got, pass_s.at[it, k - 1], pass_r.at[it, k - 1], *on_side(m)
                ).start()

    def gather_mate(it):
        rest = plane(it, 0).at[pl.ds(0, nq - 1)]
        remote(rest, rest, side_s.at[it], side_r.at[it], *on_side(1)).wait()
        mate(it, 0).start()

    def gather_end(it):
        for k in hops(nz):
            rest = plane(it, k).at[pl.ds(0, nq - 1)]
            remote(
                rest, rest, pass_s.at[it, k - 1], pass_r.at[it, k - 1], *on_side(1)
            ).wait()
            mate(it, k).start()
        whole = gath[it].at[core]
        remote(whole, whole, mate_s.at[it], mate_r.at[it], partner, me_x).wait()

    def coeffs(ts):
        acc = jnp.zeros((2 * bs, 2 * cols), F32)
        for t in ts:
            x = jnp.concatenate([ur[2 * t], ur[2 * t + 1]], axis=1)
            acc = acc + dot_nt(bw[t], x)
        return acc

    def set_coeffs(it, acc):
        acc = acc[:bs] + acc[bs:]
        gath[it][core, hz, q] = (acc[:, :cols] + acc[:, cols:]).T

    def pick(u, b):
        return jnp.concatenate([u[b], u[oidx[0, b]], u[oidx[1, b]]], axis=1)

    def row(u, b):
        return fold(dot_nn(pick(u, b), w[b]))

    BATCH = 5

    def middle(u, emit, lo=1, hi=None):
        hi = nb - 1 if hi is None else hi
        for first in range(lo, hi, BATCH):
            rows = list(range(first, min(first + BATCH, hi)))
            emit(rows, [row(u, b) for b in rows])

    def first_last(u):
        y0 = row(u, 0) + fold(dot_nn(u[left], wc[0]))
        y1 = row(u, nb - 1) + fold(dot_nn(u[right], wc[1]))
        return y0, y1

    def outer(u):
        yl = fold(dot_nn(jnp.concatenate([u[left], u[0]], axis=1), wt[0]))
        yr = fold(dot_nn(jnp.concatenate([u[right], u[nb - 1]], axis=1), wt[1]))
        return yl, yr

    coefs = cheb_coefs()

    def emit_step(k, unew):
        ca, cc = coefs[k]

        def emit(rows, ys):
            out = []
            for b, y in zip(rows, ys):
                rv = r[b]
                if k == 0:
                    dv = rv * (1.0 / THETA)
                    zv = dv
                    y = y * (1.0 / THETA)
                else:
                    dv = d[b]
                    zv = z[b]
                dv = ca * dv + cc * (rv - y)
                out.append((dv, zv + dv))
            for b, (dv, zv) in zip(rows, out):
                if k + 2 < ORDER:
                    d[b] = dv
                    put(unew, b, zv)
                z[b] = zv

        return emit

    def ends_step(k, u, unew):
        yl, yr = outer(u)
        y0, y1 = first_last(u)
        emit_step(k, unew)([0, nb - 1, left, right], [y0, y1, yl, yr])

    def outer_operator():
        wait_both(op_both)
        for side in range(2):
            for j in range(2):
                hi, lo = halves(op_in[side, j])
                wt[side, j * bs : (j + 1) * bs, 0:bs] = hi.T
                wt[side, j * bs : (j + 1) * bs, bs : 2 * bs] = lo.T

    def iteration(it):
        last = it + 1 == ITERS
        if it > 0:
            middle(ur, emit_step(0, ua))
        wait_both(functools.partial(r_copy, it))
        for side, b in ((0, left), (1, right)):
            v = r_in[it, side]
            r[b] = v
            put(ur, b, v)
        ends_step(0, ur, ua)
        gather_relay(it)
        ends_step(1, ua, ub)
        middle(ua, emit_step(1, ub))
        ends_step(2, ub, ua)
        middle(ub, emit_step(2, ua))
        ends_step(3, ua, ub)
        e_out[it, 1, 0] = z[left]
        e_out[it, 1, 1] = z[0]
        e_out[it, 0, 0] = z[right]
        e_out[it, 0, 1] = z[nb - 1]
        start_both(functools.partial(e_copy, it))
        middle(ua, emit_step(3, ub))
        gather_mate(it)
        gather_end(it)

        xs = []
        for j in range(ncb):
            g = cidx[j]
            s = g // nc
            hi, lo = halves(
                gath[it][
                    lax.rem(s, 2), s // 2 // ny, lax.rem(s // 2, ny) * nc + lax.rem(g, nc)
                ]
            )
            xs.append(jnp.concatenate([hi, lo], axis=0))
        csol = fold(dot_nn(jnp.concatenate(xs, axis=1), cw[...]))
        hi, lo = halves(csol)
        cx = jnp.concatenate([hi, lo], axis=0)
        cx = jnp.concatenate([cx, cx], axis=1)

        def spread(t):
            o = dot_nn(cx, bw[t])
            o = o[:cols] + o[cols:]
            return o[:, :bs], o[:, bs:]

        def keep(b, v):
            put(ub, b, v)
            (second_sum if last else first_sum)[0, pl.ds(b, cols, stride=nb), :] = v

        a0, a1 = spread(0)
        b0, b1 = spread(nb2 - 1)
        a_out[it, 1] = a0
        a_out[it, 0] = b1
        start_both(functools.partial(a_copy, it))
        wait_both(functools.partial(e_copy, it))
        keep(0, z[0] + e_in[it, 0, 0] + a0)
        keep(1, z[1] + a1)
        keep(nb - 2, z[nb - 2] + b0)
        keep(nb - 1, z[nb - 1] + e_in[it, 1, 0] + b1)
        for t in range(1, nb2 - 1):
            v0, v1 = spread(t)
            keep(2 * t, z[2 * t] + v0)
            keep(2 * t + 1, z[2 * t + 1] + v1)

        def emit_res(rows, ys):
            if last:
                for b, y in zip(rows, ys):
                    second_sum[1, pl.ds(b, cols, stride=nb), :] = -y
                return
            vals = [r[b] - y for b, y in zip(rows, ys)]
            for b, v in zip(rows, vals):
                r[b] = v
                first_sum[1, pl.ds(b, cols, stride=nb), :] = v
                put(ur, b, v)

        middle(ub, emit_res)
        if not last:
            acc = coeffs(range(1, nb2 - 1))
        inner = [row(ub, 0), row(ub, nb - 1)]
        wait_both(functools.partial(a_copy, it))
        for side, b in ((0, left), (1, right)):
            hi, lo = halves(a_in[it, side] + e_in[it, side, 1] + z[b])
            x = jnp.concatenate([hi, lo], axis=0)
            inner[side] = inner[side] + fold(dot_nn(x, wc[side]))
        emit_res([0, nb - 1], inner)
        if not last:
            start_both(functools.partial(r_copy, it + 1))
            set_coeffs(it + 1, acc + coeffs((0, nb2 - 1)))
            gather_begin(it + 1)

    for t in range(nb2):
        for e in range(2):
            hi, lo = halves(f_basis[pl.ds(2 * t + e, bs, stride=nb), :])
            bw[t, 0:bs, e * bs : (e + 1) * bs] = hi
            bw[t, bs : 2 * bs, e * bs : (e + 1) * bs] = lo
    set_coeffs(0, coeffs(range(nb2)))
    gather_begin(0)
    ld[2].wait()
    for j in range(2):
        hi, lo = halves(f_couple[j])
        wc[j, :, 0:bs] = hi.T
        wc[j, :, bs : 2 * bs] = lo.T

    ld[4].wait()
    ld[5].wait()
    step0 = emit_step(0, ua)
    for c in range(CHUNKS):
        both = pl.ds(0, 3 * chunk)
        pltpu.make_async_copy(diag.at[both], f_diag.at[both], wsem.at[c]).wait()
        rows, ys = [], []
        for b in range(c * chunk, (c + 1) * chunk):
            parts = []
            for v in (f_diag[b], f_offs[b, 0], f_offs[b, 1]):
                hi, lo = halves(v)
                parts.append(jnp.concatenate([hi.T, lo.T], axis=1))
            wv = jnp.concatenate(parts, axis=0)
            w[b] = wv
            if 0 < b < nb - 1:
                rows.append(b)
                ys.append(fold(dot_nn(pick(ur, b), wv)))
            if len(rows) == 4 or b == (c + 1) * chunk - 1:
                step0(rows, ys)
                rows, ys = [], []
    outer_operator()

    ld[3].wait()
    for j in range(ncb):
        hi, lo = halves(f_cblk[j])
        cw[j * bs : (j + 1) * bs, 0:bs] = hi.T
        cw[j * bs : (j + 1) * bs, bs : 2 * bs] = lo.T
    for it in range(ITERS):
        iteration(it)


def per_device(ns, nc, loads, diag, offs, oidx, couple, basis, cblk, cidx):
    _, cols, nb, bs = loads.shape
    k = basis.shape[1]
    ncb = cblk.shape[1]
    ny = 2 if ns % 4 == 0 else 1
    nz = ns // 2 // ny
    nq = ny * nc
    anyspace = pl.BlockSpec(memory_space=pl.ANY)
    vmem = pl.BlockSpec(memory_space=pltpu.VMEM)
    field = (nb + 2, cols, bs)
    ufield = (nb + 2, 2 * cols, bs)
    dma = pltpu.SemaphoreType.DMA
    out = pltpu.VMEM((2, cols * nb, bs), F32)
    first, second = pl.pallas_call(
        functools.partial(kernel, ns, nc, ny, nb, cols, bs, ncb),
        out_shape=(out, out),
        in_specs=[anyspace] * 8,
        out_specs=(vmem, vmem),
        scratch_shapes=[
            pltpu.SMEM((2, nb), jnp.int32),
            pltpu.SMEM((ncb,), jnp.int32),
            pltpu.VMEM((cols * nb, bs), F32),
            pltpu.VMEM((nb, bs, bs), F32),
            pltpu.VMEM((nb, 2, bs, bs), F32),
            pltpu.VMEM((2, bs, bs), F32),
            pltpu.VMEM((k * nb, bs), F32),
            pltpu.VMEM((ncb, bs, bs), F32),
            pltpu.VMEM((nb, 3 * bs, 2 * bs), BF16),
            pltpu.VMEM((2, bs, 2 * bs), BF16),
            pltpu.VMEM((2, 2 * bs, 2 * bs), BF16),
            pltpu.VMEM((nb // 2, 2 * bs, 2 * bs), BF16),
            pltpu.VMEM((ncb * bs, 2 * bs), BF16),
            pltpu.VMEM(field, F32),
            pltpu.VMEM(field, F32),
            pltpu.VMEM(field, F32),
            pltpu.VMEM(ufield, BF16),
            pltpu.VMEM(ufield, BF16),
            pltpu.VMEM(ufield, BF16),
            pltpu.VMEM((2, nz, nq, cols, bs), F32),
            pltpu.VMEM((2, nz, nq, cols, bs), F32),
            pltpu.VMEM((2, 2, bs, bs), F32),
            pltpu.VMEM((ITERS, 2, cols, bs), F32),
            pltpu.VMEM((ITERS, 2, 2, cols, bs), F32),
            pltpu.VMEM((ITERS, 2, 2, cols, bs), F32),
            pltpu.VMEM((ITERS, 2, cols, bs), F32),
            pltpu.VMEM((ITERS, 2, cols, bs), F32),
            dma((6,)),
            dma((CHUNKS,)),
            dma((2,)),
            dma((2,)),
            dma((ITERS, 2)),
            dma((ITERS, 2)),
            dma((ITERS, 2)),
            dma((ITERS, 2)),
            dma((ITERS, 2)),
            dma((ITERS, 2)),
            dma((ITERS, max(nz - 1, 1))),
            dma((ITERS, max(nz - 1, 1))),
            dma((ITERS,)),
            dma((ITERS,)),
            dma((ITERS, max(nz - 1, 1))),
            dma((ITERS, max(nz - 1, 1))),
            dma((ITERS,)),
            dma((ITERS,)),
        ],
        compiler_params=pltpu.CompilerParams(
            collective_id=0, has_side_effects=True, vmem_limit_bytes=56 * 1024 * 1024
        ),
    )(
        loads.reshape(cols * nb, bs), diag[0], offs[0], oidx[0].T, couple[0],
        basis.reshape(k * nb, bs), cblk[0], cidx[0],
    )
    total = first + second
    shape = (1, cols, nb, bs)
    return total[0].reshape(shape), total[1].reshape(shape)


def solution(mesh):
    lead = ("sub", "coarse")
    in_specs = (
        P(lead, None, None, None),
        P(lead, None, None, None),
        P(lead, None, None, None, None),
        P(lead, None, None),
        P(lead, None, None, None),
        P(lead, None, None, None),
        P(lead, None, None, None),
        P(lead, None),
    )
    out_specs = (P(lead, None, None, None), P(lead, None, None, None))
    return jax.shard_map(
        functools.partial(per_device, mesh.shape["sub"], mesh.shape["coarse"]),
        mesh=mesh, in_specs=in_specs, out_specs=out_specs, check_vma=False,
    )
```

```python
import functools

import jax
import jax.numpy as jnp
from jax import lax
from jax.experimental import pallas as pl
from jax.experimental.pallas import tpu as pltpu
from jax.sharding import PartitionSpec as P

ORDER = 5
ITERS = 2
THETA = 5.0
DELTA = 4.0
F32 = jnp.float32
BF16 = jnp.bfloat16
MESH = pl.DeviceIdType.MESH
CHUNKS = 2


def cheb_coefs():
    sigma = THETA / DELTA
    rho = 1.0 / sigma
    out = []
    for _ in range(ORDER - 1):
        nxt = 1.0 / (2.0 * sigma - rho)
        out.append((nxt * rho, 2.0 * nxt / DELTA))
        rho = nxt
    return out


def hops(n):
    return sorted(range(1, n), key=lambda k: min(k, n - k))


def halves(v):
    hi = v.astype(BF16)
    lo = (v - hi.astype(F32)).astype(BF16)
    return hi, lo


def dot_nt(x, w):
    return lax.dot_general(x, w, (((1,), (1,)), ((), ())), preferred_element_type=F32)


def dot_nn(x, w):
    return lax.dot_general(x, w, (((1,), (0,)), ((), ())), preferred_element_type=F32)


def kernel(
    ns, nc, ny, nb, cols, bs, ncb,
    loads, diag, offs, oidx_any, couple, basis, cblk, cidx_any,
    first_sum, second_sum,
    oidx, cidx,
    f_loads, f_diag, f_offs, f_couple, f_basis, f_cblk,
    w, wc, wt, bw, cw,
    r, d, z, ua, ub, ur,
    gath0, gath1, op_in, r_in, e_in, e_out, a_in, a_out,
    lsem, wsem, op_s, op_r, rh_s, rh_r, e_s, e_r, a_s, a_r,
    line_s, line_r, side_s, side_r, pass_s, pass_r, mate_s, mate_r,
):
    me_s = lax.axis_index("sub")
    me_x = lax.axis_index("coarse")
    core = lax.rem(me_s, 2)
    h = me_s // 2
    nz = ns // 2 // ny
    nq = ny * nc
    hz = h // ny
    q = lax.rem(h, ny) * nc + me_x
    partner = me_s + 1 - 2 * core
    has_l = me_s > 0
    has_r = me_s < ns - 1
    nb2 = nb // 2
    left, right = nb, nb + 1
    chunk = nb // CHUNKS

    ld = [
        pltpu.make_async_copy(loads, f_loads, lsem.at[0]),
        pltpu.make_async_copy(basis, f_basis, lsem.at[1]),
        pltpu.make_async_copy(couple, f_couple, lsem.at[2]),
        pltpu.make_async_copy(cblk, f_cblk, lsem.at[3]),
        pltpu.make_async_copy(oidx_any, oidx, lsem.at[4]),
        pltpu.make_async_copy(cidx_any, cidx, lsem.at[5]),
    ]
    ldw = [
        [
            pltpu.make_async_copy(src.at[span], dst.at[span], wsem.at[c])
            for src, dst in ((diag, f_diag), (offs, f_offs))
        ]
        for c, span in enumerate(pl.ds(c * chunk, chunk) for c in range(CHUNKS))
    ]
    for c in (ld[0], ld[1], ld[4], ld[5], ld[2]):
        c.start()

    def remote(src, dst, ss, rs, s, x):
        return pltpu.make_async_remote_copy(
            src_ref=src, dst_ref=dst, send_sem=ss, recv_sem=rs,
            device_id={"sub": s, "coarse": x}, device_id_type=MESH,
        )

    barrier = pltpu.get_barrier_semaphore()

    def greet(s, x):
        pl.semaphore_signal(
            barrier, inc=1, device_id={"sub": s, "coarse": x}, device_id_type=MESH
        )

    def on_line(k):
        return core + 2 * (lax.rem(hz + k, nz) * ny + lax.rem(h, ny)), me_x

    def on_side(m):
        to = lax.rem(q + m, nq)
        return core + 2 * (hz * ny + to // nc), lax.rem(to, nc)

    for k in range(1, nz):
        greet(*on_line(k))
    for m in range(1, nq):
        greet(*on_side(m))

    @pl.when(has_l)
    def _():
        greet(me_s - 1, me_x)

    @pl.when(has_r)
    def _():
        greet(me_s + 1, me_x)

    for side, has in ((0, has_l), (1, has_r)):

        @pl.when(jnp.logical_not(has))
        def _():
            op_in[side] = jnp.zeros_like(op_in[side])
            for it in range(ITERS):
                r_in[it, side] = jnp.zeros_like(r_in[it, side])
                e_in[it, side] = jnp.zeros_like(e_in[it, side])
                a_in[it, side] = jnp.zeros_like(a_in[it, side])

    def put(ref, b, v):
        hi, lo = halves(v)
        ref[b, 0:cols, :] = hi
        ref[b, cols : 2 * cols, :] = lo

    def fold(o):
        return (o[:cols, :bs] + o[:cols, bs:]) + (o[cols:, :bs] + o[cols:, bs:])

    ld[0].wait()

    for b in range(nb):
        v = f_loads[pl.ds(b, cols, stride=nb), :]
        r[b] = v
        put(ur, b, v)
    pl.semaphore_wait(
        barrier, nz - 1 + nq - 1 + has_l.astype(jnp.int32) + has_r.astype(jnp.int32)
    )

    def op_copies(to_left):
        b = 0 if to_left else nb - 1
        side = 1 if to_left else 0
        s = me_s - 1 if to_left else me_s + 1
        return [
            remote(diag.at[b], op_in.at[side, 0], op_s.at[side], op_r.at[side], s, me_x),
            remote(
                couple.at[0 if to_left else 1], op_in.at[side, 1],
                op_s.at[side], op_r.at[side], s, me_x,
            ),
        ]

    def op_both(to_left):
        side = 1 if to_left else 0
        s = me_s - 1 if to_left else me_s + 1
        return [remote(op_in.at[side], op_in.at[side], op_s.at[side], op_r.at[side], s, me_x)]

    def r_copy(it, to_left):
        b = 0 if to_left else nb - 1
        side = 1 if to_left else 0
        s = me_s - 1 if to_left else me_s + 1
        return [remote(r.at[b], r_in.at[it, side], rh_s.at[it, side], rh_r.at[it, side], s, me_x)]

    def e_copy(it, to_left):
        side = 1 if to_left else 0
        s = me_s - 1 if to_left else me_s + 1
        return [
            remote(
                e_out.at[it, side], e_in.at[it, side], e_s.at[it, side], e_r.at[it, side], s, me_x
            )
        ]

    def a_copy(it, to_left):
        side = 1 if to_left else 0
        s = me_s - 1 if to_left else me_s + 1
        return [
            remote(
                a_out.at[it, side], a_in.at[it, side], a_s.at[it, side], a_r.at[it, side], s, me_x
            )
        ]

    def start_both(make):
        @pl.when(has_l)
        def _():
            for c in make(True):
                c.start()

        @pl.when(has_r)
        def _():
            for c in make(False):
                c.start()

    def wait_both(make):
        @pl.when(has_l)
        def _():
            for c in make(True):
                c.wait_send()
            for c in make(False):
                c.wait_recv()

        @pl.when(has_r)
        def _():
            for c in make(False):
                c.wait_send()
            for c in make(True):
                c.wait_recv()

    start_both(functools.partial(r_copy, 0))
    start_both(op_copies)
    ld[1].wait()
    for pair in ldw:
        for c in pair:
            c.start()
    ld[3].start()

    gath = (gath0, gath1)

    def plane(it, k):
        return gath[it].at[core, lax.rem(hz - k + nz, nz)]

    def line(it, k):
        mine = gath[it].at[core, hz, q]
        return remote(mine, mine, line_s.at[it, k - 1], line_r.at[it, k - 1], *on_line(k))

    def mate(it, k):
        return remote(plane(it, k), plane(it, k), mate_s.at[it], mate_r.at[it], partner, me_x)

    def gather_begin(it):
        for k in hops(nz):
            line(it, k).start()
        mine = gath[it].at[core, hz, q]
        for m in range(1, nq):
            remote(mine, mine, side_s.at[it], side_r.at[it], *on_side(m)).start()

    def gather_relay(it):
        for k in hops(nz):
            line(it, k).wait()
            got = plane(it, k).at[q]
            for m in range(1, nq):
                remote(
                    got, got, pass_s.at[it, k - 1], pass_r.at[it, k - 1], *on_side(m)
                ).start()

    def gather_mate(it):
        rest = plane(it, 0).at[pl.ds(0, nq - 1)]
        remote(rest, rest, side_s.at[it], side_r.at[it], *on_side(1)).wait()
        mate(it, 0).start()

    def gather_end(it):
        for k in hops(nz):
            rest = plane(it, k).at[pl.ds(0, nq - 1)]
            remote(
                rest, rest, pass_s.at[it, k - 1], pass_r.at[it, k - 1], *on_side(1)
            ).wait()
            mate(it, k).start()
        whole = gath[it].at[core]
        remote(whole, whole, mate_s.at[it], mate_r.at[it], partner, me_x).wait()

    def coeffs(ts):
        acc = jnp.zeros((2 * bs, 2 * cols), F32)
        for t in ts:
            x = jnp.concatenate([ur[2 * t], ur[2 * t + 1]], axis=1)
            acc = acc + dot_nt(bw[t], x)
        return acc

    def set_coeffs(it, acc):
        acc = acc[:bs] + acc[bs:]
        gath[it][core, hz, q] = (acc[:, :cols] + acc[:, cols:]).T

    def pick(u, b):
        return jnp.concatenate([u[b], u[oidx[0, b]], u[oidx[1, b]]], axis=1)

    def row(u, b):
        return fold(dot_nn(pick(u, b), w[b]))

    BATCH = 3

    def middle(u, emit, lo=1, hi=None):
        hi = nb - 1 if hi is None else hi
        for first in range(lo, hi, BATCH):
            rows = list(range(first, min(first + BATCH, hi)))
            emit(rows, [row(u, b) for b in rows])

    def first_last(u):
        y0 = row(u, 0) + fold(dot_nn(u[left], wc[0]))
        y1 = row(u, nb - 1) + fold(dot_nn(u[right], wc[1]))
        return y0, y1

    def outer(u):
        yl = fold(dot_nn(jnp.concatenate([u[left], u[0]], axis=1), wt[0]))
        yr = fold(dot_nn(jnp.concatenate([u[right], u[nb - 1]], axis=1), wt[1]))
        return yl, yr

    coefs = cheb_coefs()

    def emit_step(k, unew):
        ca, cc = coefs[k]

        def emit(rows, ys):
            out = []
            for b, y in zip(rows, ys):
                rv = r[b]
                if k == 0:
                    dv = rv * (1.0 / THETA)
                    zv = dv
                    y = y * (1.0 / THETA)
                else:
                    dv = d[b]
                    zv = z[b]
                dv = ca * dv + cc * (rv - y)
                out.append((dv, zv + dv))
            for b, (dv, zv) in zip(rows, out):
                if k + 2 < ORDER:
                    d[b] = dv
                    put(unew, b, zv)
                z[b] = zv

        return emit

    def ends_step(k, u, unew):
        yl, yr = outer(u)
        y0, y1 = first_last(u)
        emit_step(k, unew)([0, nb - 1, left, right], [y0, y1, yl, yr])

    def outer_operator():
        wait_both(op_both)
        for side in range(2):
            for j in range(2):
                hi, lo = halves(op_in[side, j])
                wt[side, j * bs : (j + 1) * bs, 0:bs] = hi.T
                wt[side, j * bs : (j + 1) * bs, bs : 2 * bs] = lo.T

    def iteration(it):
        last = it + 1 == ITERS
        if it > 0:
            middle(ur, emit_step(0, ua))
        wait_both(functools.partial(r_copy, it))
        for side, b in ((0, left), (1, right)):
            v = r_in[it, side]
            r[b] = v
            put(ur, b, v)
        ends_step(0, ur, ua)
        gather_relay(it)
        gather_mate(it)
        ends_step(1, ua, ub)
        middle(ua, emit_step(1, ub))
        ends_step(2, ub, ua)
        middle(ub, emit_step(2, ua))
        ends_step(3, ua, ub)
        e_out[it, 1, 0] = z[left]
        e_out[it, 1, 1] = z[0]
        e_out[it, 0, 0] = z[right]
        e_out[it, 0, 1] = z[nb - 1]
        start_both(functools.partial(e_copy, it))
        middle(ua, emit_step(3, ub))
        gather_end(it)

        xs = []
        for j in range(ncb):
            g = cidx[j]
            s = g // nc
            hi, lo = halves(
                gath[it][
                    lax.rem(s, 2), s // 2 // ny, lax.rem(s // 2, ny) * nc + lax.rem(g, nc)
                ]
            )
            xs.append(jnp.concatenate([hi, lo], axis=0))
        csol = fold(dot_nn(jnp.concatenate(xs, axis=1), cw[...]))
        hi, lo = halves(csol)
        cx = jnp.concatenate([hi, lo], axis=0)
        cx = jnp.concatenate([cx, cx], axis=1)

        def spread(t):
            o = dot_nn(cx, bw[t])
            o = o[:cols] + o[cols:]
            return o[:, :bs], o[:, bs:]

        def keep(b, v):
            put(ub, b, v)
            (second_sum if last else first_sum)[0, pl.ds(b, cols, stride=nb), :] = v

        a0, a1 = spread(0)
        b0, b1 = spread(nb2 - 1)
        a_out[it, 1] = a0
        a_out[it, 0] = b1
        start_both(functools.partial(a_copy, it))
        wait_both(functools.partial(e_copy, it))
        keep(0, z[0] + e_in[it, 0, 0] + a0)
        keep(1, z[1] + a1)
        keep(nb - 2, z[nb - 2] + b0)
        keep(nb - 1, z[nb - 1] + e_in[it, 1, 0] + b1)
        for t in range(1, nb2 - 1):
            v0, v1 = spread(t)
            keep(2 * t, z[2 * t] + v0)
            keep(2 * t + 1, z[2 * t + 1] + v1)

        def emit_res(rows, ys):
            if last:
                for b, y in zip(rows, ys):
                    second_sum[1, pl.ds(b, cols, stride=nb), :] = -y
                return
            vals = [r[b] - y for b, y in zip(rows, ys)]
            for b, v in zip(rows, vals):
                r[b] = v
                first_sum[1, pl.ds(b, cols, stride=nb), :] = v
                put(ur, b, v)

        middle(ub, emit_res)
        if not last:
            acc = coeffs(range(1, nb2 - 1))
        inner = [row(ub, 0), row(ub, nb - 1)]
        wait_both(functools.partial(a_copy, it))
        for side, b in ((0, left), (1, right)):
            hi, lo = halves(a_in[it, side] + e_in[it, side, 1] + z[b])
            x = jnp.concatenate([hi, lo], axis=0)
            inner[side] = inner[side] + fold(dot_nn(x, wc[side]))
        emit_res([0, nb - 1], inner)
        if not last:
            start_both(functools.partial(r_copy, it + 1))
            set_coeffs(it + 1, acc + coeffs((0, nb2 - 1)))
            gather_begin(it + 1)

    for t in range(nb2):
        for e in range(2):
            hi, lo = halves(f_basis[pl.ds(2 * t + e, bs, stride=nb), :])
            bw[t, 0:bs, e * bs : (e + 1) * bs] = hi
            bw[t, bs : 2 * bs, e * bs : (e + 1) * bs] = lo
    set_coeffs(0, coeffs(range(nb2)))
    gather_begin(0)
    ld[2].wait()
    for j in range(2):
        hi, lo = halves(f_couple[j])
        wc[j, :, 0:bs] = hi.T
        wc[j, :, bs : 2 * bs] = lo.T

    ld[4].wait()
    ld[5].wait()
    step0 = emit_step(0, ua)
    for c in range(CHUNKS):
        both = pl.ds(0, 3 * chunk // 2)
        pltpu.make_async_copy(offs.at[both], f_offs.at[both], wsem.at[c]).wait()
        rows, ys = [], []
        for b in range(c * chunk, (c + 1) * chunk):
            parts = []
            for v in (f_diag[b], f_offs[b, 0], f_offs[b, 1]):
                hi, lo = halves(v)
                parts.append(jnp.concatenate([hi.T, lo.T], axis=1))
            wv = jnp.concatenate(parts, axis=0)
            w[b] = wv
            if 0 < b < nb - 1:
                rows.append(b)
                ys.append(fold(dot_nn(pick(ur, b), wv)))
            if len(rows) == 8 or b == (c + 1) * chunk - 1:
                step0(rows, ys)
                rows, ys = [], []
    outer_operator()

    ld[3].wait()
    for j in range(ncb):
        hi, lo = halves(f_cblk[j])
        cw[j * bs : (j + 1) * bs, 0:bs] = hi.T
        cw[j * bs : (j + 1) * bs, bs : 2 * bs] = lo.T
    for it in range(ITERS):
        iteration(it)


def per_device(ns, nc, loads, diag, offs, oidx, couple, basis, cblk, cidx):
    _, cols, nb, bs = loads.shape
    k = basis.shape[1]
    ncb = cblk.shape[1]
    ny = 2 if ns % 4 == 0 else 1
    nz = ns // 2 // ny
    nq = ny * nc
    anyspace = pl.BlockSpec(memory_space=pl.ANY)
    vmem = pl.BlockSpec(memory_space=pltpu.VMEM)
    field = (nb + 2, cols, bs)
    ufield = (nb + 2, 2 * cols, bs)
    dma = pltpu.SemaphoreType.DMA
    out = pltpu.VMEM((2, cols * nb, bs), F32)
    first, second = pl.pallas_call(
        functools.partial(kernel, ns, nc, ny, nb, cols, bs, ncb),
        out_shape=(out, out),
        in_specs=[anyspace] * 8,
        out_specs=(vmem, vmem),
        scratch_shapes=[
            pltpu.SMEM((2, nb), jnp.int32),
            pltpu.SMEM((ncb,), jnp.int32),
            pltpu.VMEM((cols * nb, bs), F32),
            pltpu.VMEM((nb, bs, bs), F32),
            pltpu.VMEM((nb, 2, bs, bs), F32),
            pltpu.VMEM((2, bs, bs), F32),
            pltpu.VMEM((k * nb, bs), F32),
            pltpu.VMEM((ncb, bs, bs), F32),
            pltpu.VMEM((nb, 3 * bs, 2 * bs), BF16),
            pltpu.VMEM((2, bs, 2 * bs), BF16),
            pltpu.VMEM((2, 2 * bs, 2 * bs), BF16),
            pltpu.VMEM((nb // 2, 2 * bs, 2 * bs), BF16),
            pltpu.VMEM((ncb * bs, 2 * bs), BF16),
            pltpu.VMEM(field, F32),
            pltpu.VMEM(field, F32),
            pltpu.VMEM(field, F32),
            pltpu.VMEM(ufield, BF16),
            pltpu.VMEM(ufield, BF16),
            pltpu.VMEM(ufield, BF16),
            pltpu.VMEM((2, nz, nq, cols, bs), F32),
            pltpu.VMEM((2, nz, nq, cols, bs), F32),
            pltpu.VMEM((2, 2, bs, bs), F32),
            pltpu.VMEM((ITERS, 2, cols, bs), F32),
            pltpu.VMEM((ITERS, 2, 2, cols, bs), F32),
            pltpu.VMEM((ITERS, 2, 2, cols, bs), F32),
            pltpu.VMEM((ITERS, 2, cols, bs), F32),
            pltpu.VMEM((ITERS, 2, cols, bs), F32),
            dma((6,)),
            dma((CHUNKS,)),
            dma((2,)),
            dma((2,)),
            dma((ITERS, 2)),
            dma((ITERS, 2)),
            dma((ITERS, 2)),
            dma((ITERS, 2)),
            dma((ITERS, 2)),
            dma((ITERS, 2)),
            dma((ITERS, max(nz - 1, 1))),
            dma((ITERS, max(nz - 1, 1))),
            dma((ITERS,)),
            dma((ITERS,)),
            dma((ITERS, max(nz - 1, 1))),
            dma((ITERS, max(nz - 1, 1))),
            dma((ITERS,)),
            dma((ITERS,)),
        ],
        compiler_params=pltpu.CompilerParams(
            collective_id=0, has_side_effects=True, vmem_limit_bytes=56 * 1024 * 1024
        ),
    )(
        loads.reshape(cols * nb, bs), diag[0], offs[0], oidx[0].T, couple[0],
        basis.reshape(k * nb, bs), cblk[0], cidx[0],
    )
    total = first + second
    shape = (1, cols, nb, bs)
    return total[0].reshape(shape), total[1].reshape(shape)


def solution(mesh):
    lead = ("sub", "coarse")
    in_specs = (
        P(lead, None, None, None),
        P(lead, None, None, None),
        P(lead, None, None, None, None),
        P(lead, None, None),
        P(lead, None, None, None),
        P(lead, None, None, None),
        P(lead, None, None, None),
        P(lead, None),
    )
    out_specs = (P(lead, None, None, None), P(lead, None, None, None))
    return jax.shard_map(
        functools.partial(per_device, mesh.shape["sub"], mesh.shape["coarse"]),
        mesh=mesh, in_specs=in_specs, out_specs=out_specs, check_vma=False,
    )
```
